128 devices in a mesh: tile: 32 (over x, z, core), dp: 4 (over y).
Axes of the slice: x: 4, y: 4, z: 4, core: 2. Of those that a mesh axis runs over, the one named last changes fastest.
Arguments:
- fields: bfloat16 [4, 64, 64, 64, 128], P('dp', 'tile'), may hold values from -6 to 6
- cotangent: bfloat16 [4, 64, 64, 64, 128], P('dp', 'tile'), may hold values from -6 to 6
- is_ocean: int32 [64], P('tile'), may hold values from 0 to 1, as said below
- neighbours: int32 [64, 8], P('tile'), may hold values from -1 to 63, as said below
- kernel: float32 [7, 7, 128], replicated, may hold values from -0.875 to 0.875
- conv_bias: float32 [128], replicated, may hold values from -3 to 3
- ln_gain: float32 [128], replicated, may hold values from 0.25 to 1.75
- ln_bias: float32 [128], replicated, may hold values from -3 to 3
- w_up: bfloat16 [128, 512], replicated, may hold values from -0.5 to 0.5
- up_bias: float32 [512], replicated, may hold values from -3 to 3
- w_down: bfloat16 [512, 128], replicated, may hold values from -0.25 to 0.25
- down_bias: float32 [128], replicated, may hold values from -3 to 3
- layer_scale: float32 [128], replicated, may hold values from 0.3 to 1
Outputs:
- grad_fields: bfloat16 [4, 64, 64, 64, 128], P('dp', 'tile')
- g_kernel: float32 [7, 7, 128], replicated
- g_conv_bias: float32 [128], replicated
- g_ln_gain: float32 [128], replicated
- g_ln_bias: float32 [128], replicated
- g_w_up: float32 [128, 512], replicated
- g_up_bias: float32 [512], replicated
- g_w_down: float32 [512, 128], replicated
- g_down_bias: float32 [128], replicated
- g_layer_scale: float32 [128], replicated
The draws below stay inside these ranges and needn't reach their ends.
Inputs may be any that keep to these rules, and one draw needn't show every extreme that they name: `is_ocean`: slots follow a serpentine curve through the columns of a grid of 8 x 8 tiles, alternating direction from column to column; tiles of the first and last grid rows are ocean. Entry k of slot s names the slot of the tile adjacent in direction k (north, south, west, east, north-west, north-east, south-west, south-east), or -1 where that tile is land or outside the grid or slot s is land; the relation is symmetric; the north and south neighbours are slot s - 1 or s + 1, and every neighbour lies within 15 slots of s.
All inputs are finite; a program needn't handle non-finite values.
Results may differ from the reference program's by a relative error of at most 0.0071.
Values may be sent and summed in bfloat16 or wider, within the bound.
No kernel may reach another device: no remote copies, remote signals or barrier semaphores. Data moves between devices by JAX's collectives and lax.ppermute only.
A program may use at most 128 MiB of HBM per device.

```python
import math
import jax
import jax.numpy as jnp
from jax import lax

CH = 128
HIDDEN_SIZE = 512
TILE = 64
TROWS = 8
SLOTS = 64
TCOLS = 8
SAMPLES = 4


def plan_draw(key):
    base_key = jax.random.fold_in(key, 7321)
    land_key, flip_key, row_key, column_key = jax.random.split(base_key, 4)
    land_mask = jax.random.randint(land_key, (TROWS, TCOLS), 0, 4) == 0
    row_ids = jnp.arange(TROWS)[:, None]
    column_ids = jnp.arange(TCOLS)[None, :]
    forced_row = jax.random.randint(row_key, (), 1, TROWS - 1)
    forced_column = jax.random.randint(column_key, (), 0, TCOLS)
    land_mask = land_mask | (row_ids == forced_row) & (column_ids == forced_column)
    land_mask = land_mask & (row_ids > 0) & (row_ids < TROWS - 1)
    flip_bit = jax.random.randint(flip_key, (), 0, 2)
    downward = (jnp.arange(TCOLS) + flip_bit) % 2 == 0
    slot_ids = jnp.arange(SLOTS)
    column = slot_ids // TROWS
    along = slot_ids % TROWS
    grid_row = jnp.where(downward[column], along, TROWS - 1 - along)
    ocean = jnp.logical_not(land_mask[grid_row, column])
    offsets = [(-1, 0), (1, 0), (0, -1), (0, 1), (-1, -1), (-1, 1), (1, -1), (1, 1)]
    columns_out = []
    for row_step, col_step in offsets:
        target_row = grid_row + row_step
        target_column = column + col_step
        inside = (target_row >= 0) & (target_row < TROWS) & (target_column >= 0) & (target_column < TCOLS)
        clipped_row = jnp.clip(target_row, 0, TROWS - 1)
        clipped_column = jnp.clip(target_column, 0, TCOLS - 1)
        linked = inside & jnp.logical_not(land_mask[clipped_row, clipped_column]) & ocean
        target_slot = clipped_column * TROWS + jnp.where(downward[clipped_column], clipped_row, TROWS - 1 - clipped_row)
        columns_out.append(jnp.where(linked, target_slot, -1))
    return (ocean.astype(jnp.int32), jnp.stack(columns_out, 1).astype(jnp.int32))


def draw_is_ocean(key, part):
    return plan_draw(key)[0]


def draw_neighbours(key, part):
    return plan_draw(key)[1]


def block_scale(stream_key, shape, shards, smallest, high):
    def one(axis_at, shards_of):
        steps = jax.random.uniform(jax.random.fold_in(jax.random.fold_in(stream_key, 6), axis_at), (shards_of,), jnp.float32, smallest / len(shards), high / len(shards))
        return jnp.repeat(jnp.exp(steps), shape[axis_at] // shards_of).reshape((-1,) + (1,) * (len(shape) - axis_at - 1))

    factor_of = one(*shards[0])
    for cut in shards[1:]:
        factor_of = factor_of * one(*cut)
    return factor_of


def bell_draw(own_key, shape, scale, most, pieces=(), held_as=jnp.bfloat16):
    values = scale * jax.random.normal(own_key, shape, jnp.float32)
    if pieces:
        values = values * block_scale(own_key, shape, pieces, -0.22, 0.18)
    return jnp.clip(values, -most, most).astype(held_as)


def setup_inputs(seed: int = 0) -> dict:
    key_of = jax.random.split(jax.random.key(seed), 14)
    fields = bell_draw(key_of[0], (SAMPLES, SLOTS, TILE, TILE, CH), 1.0, 6.0, ((0, 4), (1, 32)))
    cotangent = bell_draw(key_of[1], (SAMPLES, SLOTS, TILE, TILE, CH), 1.0, 6.0, ((0, 4), (1, 32)))
    is_ocean = draw_is_ocean(jax.random.fold_in(key_of[13], 71), 0)
    neighbours = draw_neighbours(jax.random.fold_in(key_of[13], 71), 0)
    kernel = bell_draw(key_of[4], (7, 7, CH), 49 ** -0.5, 0.875, (), jnp.float32)
    conv_bias = bell_draw(key_of[5], (CH,), 0.5, 3.0, (), jnp.float32)
    ln_gain = jnp.clip(1.0 + 0.15 * jax.random.normal(key_of[6], (CH,), jnp.float32), 0.25, 1.75)
    ln_bias = bell_draw(key_of[7], (CH,), 0.5, 3.0, (), jnp.float32)
    w_up = bell_draw(key_of[8], (CH, HIDDEN_SIZE), CH ** -0.5, 0.5)
    up_bias = bell_draw(key_of[9], (HIDDEN_SIZE,), 0.5, 3.0, (), jnp.float32)
    w_down = bell_draw(key_of[10], (HIDDEN_SIZE, CH), HIDDEN_SIZE ** -0.5, 0.25)
    down_bias = bell_draw(key_of[11], (CH,), 0.5, 3.0, (), jnp.float32)
    layer_scale = jnp.clip(jnp.exp(jax.random.uniform(key_of[12], (CH,), jnp.float32, math.log(0.3), math.log(1.0))), 0.3, 1.0)
    return {"fields": fields, "cotangent": cotangent, "is_ocean": is_ocean, "neighbours": neighbours, "kernel": kernel, "conv_bias": conv_bias, "ln_gain": ln_gain, "ln_bias": ln_bias, "w_up": w_up, "up_bias": up_bias, "w_down": w_down, "down_bias": down_bias, "layer_scale": layer_scale}


EPSILON = 1e-06

def rims_of(tile_block, rim_depth):
    extent = tile_block.shape[0]
    top_band = tile_block[:rim_depth]
    bottom = tile_block[extent - rim_depth:]
    left_band = jnp.transpose(tile_block[:, :rim_depth], (1, 0, 2))
    right_band = jnp.transpose(tile_block[:, extent - rim_depth:], (1, 0, 2))
    return jnp.stack([top_band, bottom, left_band, right_band], 0)

def assemble(own_tile, picked, valid_flags, first_layer, rim_depth):
    extent = own_tile.shape[0]

    def rim_piece(direction, which_strip):
        stripe = picked[direction][which_strip, first_layer:first_layer + rim_depth]
        return stripe * valid_flags[direction].astype(own_tile.dtype)
    north_rim = rim_piece(0, 1)
    south_rim = rim_piece(1, 0)
    west_rim = jnp.transpose(rim_piece(2, 1), (1, 0, 2))
    east_rim = jnp.transpose(rim_piece(3, 0), (1, 0, 2))
    north_west = jnp.transpose(rim_piece(4, 1)[:, extent - rim_depth:], (1, 0, 2))
    north_east = jnp.transpose(rim_piece(5, 0)[:, extent - rim_depth:], (1, 0, 2))
    south_west = jnp.transpose(rim_piece(6, 1)[:, :rim_depth], (1, 0, 2))
    south_east = jnp.transpose(rim_piece(7, 0)[:, :rim_depth], (1, 0, 2))
    top_band = jnp.concatenate([north_west, north_rim, north_east], 1)
    middle = jnp.concatenate([west_rim, own_tile, east_rim], 1)
    bottom = jnp.concatenate([south_west, south_rim, south_east], 1)
    return jnp.concatenate([top_band, middle, bottom], 0)

def depthwise(padded, kernel, extent):
    running_sum = jnp.zeros((extent, extent, padded.shape[2]), jnp.float32)
    for lag_row in range(7):
        for lag_col in range(7):
            window = padded[lag_row:lag_row + extent, lag_col:lag_col + extent].astype(jnp.float32)
            running_sum = running_sum + window * kernel[lag_row, lag_col]
    return running_sum

def transposed(grad_padded, kernel, extent):
    running_sum = jnp.zeros((extent, extent, grad_padded.shape[2]), jnp.float32)
    for lag_row in range(7):
        for lag_col in range(7):
            window = grad_padded[6 - lag_row:6 - lag_row + extent, 6 - lag_col:6 - lag_col + extent].astype(jnp.float32)
            running_sum = running_sum + window * kernel[lag_row, lag_col]
    return running_sum

def kernel_terms(grad_tile, padded, extent):
    grad_values = grad_tile.astype(jnp.float32)
    stacked = []
    for lag_row in range(7):
        line_terms = []
        for lag_col in range(7):
            window = padded[lag_row:lag_row + extent, lag_col:lag_col + extent].astype(jnp.float32)
            line_terms.append(lax.optimization_barrier(jnp.sum(grad_values * window, axis=(0, 1))))
        stacked.append(jnp.stack(line_terms, 0))
    return jnp.stack(stacked, 0)

def gelu_tanh(values):
    return jax.nn.gelu(values, approximate=True)

def layer_rows(conv_rows, cot_rows, ln_gain, ln_bias, w_up, up_bias, w_down, down_bias, layer_scale):
    mean_value = lax.optimization_barrier(jnp.mean(conv_rows, -1, keepdims=True))
    centred = conv_rows - mean_value
    variance = lax.optimization_barrier(jnp.mean(centred * centred, -1, keepdims=True))
    inverse_scale = lax.rsqrt(variance + EPSILON)
    normed = centred * inverse_scale
    scaled = (normed * ln_gain + ln_bias).astype(jnp.bfloat16)
    hidden_sum = jnp.dot(scaled, w_up, preferred_element_type=jnp.float32) + up_bias
    activation = gelu_tanh(hidden_sum).astype(jnp.bfloat16)
    mixed = jnp.dot(activation, w_down, preferred_element_type=jnp.float32) + down_bias
    grad_mixed = (cot_rows * layer_scale).astype(jnp.bfloat16)
    grad_act = jnp.dot(grad_mixed, w_down.T, preferred_element_type=jnp.float32)
    pullback = jax.vjp(gelu_tanh, hidden_sum)[1]
    grad_pre = pullback(grad_act)[0].astype(jnp.bfloat16)
    grad_scaled = jnp.dot(grad_pre, w_up.T, preferred_element_type=jnp.float32)
    grad_normed = grad_scaled * ln_gain
    grad_conv = inverse_scale * (grad_normed - lax.optimization_barrier(jnp.mean(grad_normed, -1, keepdims=True)) - normed * lax.optimization_barrier(jnp.mean(grad_normed * normed, -1, keepdims=True)))
    return (grad_conv.astype(jnp.bfloat16), mixed, grad_mixed, activation, grad_pre, scaled, grad_scaled, normed)

def row_terms(cot_rows, mixed, grad_mixed, activation, grad_pre, scaled, grad_scaled, normed, grad_conv):
    return (lax.optimization_barrier(jnp.sum(grad_conv.astype(jnp.float32), 0)), lax.optimization_barrier(jnp.sum(grad_scaled * normed, 0)), lax.optimization_barrier(jnp.sum(grad_scaled, 0)), jnp.dot(scaled.T, grad_pre, preferred_element_type=jnp.float32), lax.optimization_barrier(jnp.sum(grad_pre.astype(jnp.float32), 0)), jnp.dot(activation.T, grad_mixed, preferred_element_type=jnp.float32), lax.optimization_barrier(jnp.sum(grad_mixed.astype(jnp.float32), 0)), lax.optimization_barrier(jnp.sum(cot_rows * mixed, 0)))

def reference(fields, cotangent, is_ocean, neighbours, kernel, conv_bias, ln_gain, ln_bias, w_up, up_bias, w_down, down_bias, layer_scale):
    samples, slot_count, extent, channels = (fields.shape[0], fields.shape[1], fields.shape[2], fields.shape[4])
    hidden_width = w_up.shape[1]
    grad_sums = (jnp.zeros((7, 7, channels), jnp.float32), jnp.zeros((channels,), jnp.float32), jnp.zeros((channels,), jnp.float32), jnp.zeros((channels,), jnp.float32), jnp.zeros((channels, hidden_width), jnp.float32), jnp.zeros((hidden_width,), jnp.float32), jnp.zeros((hidden_width, channels), jnp.float32), jnp.zeros((channels,), jnp.float32), jnp.zeros((channels,), jnp.float32))
    outputs = []
    for sample in range(samples):
        tile_stack = fields[sample]
        cot_stack = cotangent[sample]
        rims_x = jax.vmap(lambda tile_block: rims_of(tile_block, 3))(tile_stack)

        def fetch_rims(rim_set, slot_ids):
            safe_ids = jnp.maximum(slot_ids, 0)
            picked = [rim_set[safe_ids[0]], rim_set[safe_ids[1]]]
            picked = picked + [rim_set[safe_ids[direction]][2:4] for direction in range(2, 8)]
            return (picked, slot_ids >= 0)

        def first_pass(running, slot_id):
            picked, valid_flags = fetch_rims(rims_x, neighbours[slot_id])
            padded = assemble(tile_stack[slot_id], picked, valid_flags, 0, 3)
            conv_out = depthwise(padded, kernel, extent) + conv_bias
            cot_rows = cot_stack[slot_id].astype(jnp.float32).reshape(-1, channels)
            layer_parts = layer_rows(conv_out.reshape(-1, channels), cot_rows, ln_gain, ln_bias, w_up, up_bias, w_down, down_bias, layer_scale)
            grad_tile = layer_parts[0].reshape(extent, extent, channels)
            weight_terms = (kernel_terms(grad_tile, padded, extent),) + row_terms(cot_rows, *layer_parts[1:], layer_parts[0])
            keep_flag = (is_ocean[slot_id] > 0).astype(jnp.float32)
            running = tuple((total + keep_flag * term for total, term in zip(running, weight_terms)))
            return (running, grad_tile)
        grad_sums, grad_all = lax.scan(first_pass, grad_sums, jnp.arange(slot_count))
        rims_g = jax.vmap(lambda tile_block: rims_of(tile_block, 3))(grad_all)

        def second_pass(slot_id):
            picked, valid_flags = fetch_rims(rims_g, neighbours[slot_id])
            grad_padded = assemble(grad_all[slot_id], picked, valid_flags, 0, 3)
            result = cot_stack[slot_id].astype(jnp.float32) + transposed(grad_padded, kernel, extent)
            keep_flag = (is_ocean[slot_id] > 0).astype(jnp.float32)
            return (result * keep_flag).astype(jnp.bfloat16)
        outputs.append(lax.map(second_pass, jnp.arange(slot_count)))
    grad_scale = 1.0 / float(samples * slot_count * extent * extent) ** 0.5
    return (jnp.stack(outputs, 0), grad_sums[0] * grad_scale, grad_sums[1] * grad_scale, grad_sums[2] * grad_scale, grad_sums[3] * grad_scale, grad_sums[4] * grad_scale, grad_sums[5] * grad_scale, grad_sums[6] * grad_scale, grad_sums[7] * grad_scale, grad_sums[8] * grad_scale)
```

```python
from functools import partial
import math

import jax
import jax.numpy as jnp
from jax import lax
from jax.experimental import pallas as pl
from jax.experimental.pallas import tpu as pltpu
from jax.sharding import PartitionSpec as P


EPSILON = 1e-06
BF = jnp.bfloat16
F32 = jnp.float32
PITCH = 80
LEFT = 5
C0 = math.sqrt(2.0 / math.pi)
C1 = 0.044715
VMEM = pltpu.VMEM
LIMIT = 60 * 1024 * 1024


RB = 8
UN = 2


def gelu_pair(h, ga):
    sq = h * h
    t = jnp.tanh(h * (C0 + (C0 * C1) * sq))
    s = 0.5 + 0.5 * t
    act = h * s
    slope = s + (act - act * s) * (2 * C0 + (6 * C0 * C1) * sq)
    return act.astype(BF), (ga * slope).astype(BF)


def vspec():
    return pl.BlockSpec(memory_space=pltpu.VMEM)


def sspec():
    return pl.BlockSpec(memory_space=pltpu.SMEM)


def call(kernel, outs, scratch, args, smem, flops=0, bytes_accessed=0, blocks=None, alias=None):
    blocks = blocks or {}
    specs = [
        sspec() if i < smem else blocks.get(i, vspec()) for i in range(len(args))
    ]
    return pl.pallas_call(
        kernel,
        out_shape=outs,
        grid=(1,) if blocks else (),
        in_specs=specs,
        out_specs=jax.tree.map(lambda _: vspec(), outs),
        scratch_shapes=scratch,
        input_output_aliases=alias or {},
        compiler_params=pltpu.CompilerParams(vmem_limit_bytes=LIMIT),
        cost_estimate=pl.CostEstimate(
            flops=flops, bytes_accessed=bytes_accessed, transcendentals=0
        ),
    )(*args)


def pack_sides(nb, west_of, east_of, to_prev, to_next, wide):
    position = lax.axis_index("tile")
    for slot in range(2):
        s = 2 * position + slot
        east_prev = jnp.bool_(False)
        east_next = jnp.bool_(False)
        for d in (3, 5, 7):
            e = nb[slot, d]
            east_prev = east_prev | ((e >= 0) & (e < s))
            east_next = east_next | (e > s)
        wide[0] = west_of(slot).astype(F32).reshape(512, 128)
        wide[1] = east_of(slot).astype(F32).reshape(512, 128)
        for j in range(3):
            west = wide[0, pl.ds(j, 64, stride=8), :]
            east = wide[1, pl.ds(5 + j, 64, stride=8), :]
            to_prev[slot, j] = jnp.where(east_prev, east, west).astype(BF)
            to_next[slot, j] = jnp.where(east_next, east, west).astype(BF)


def sides_kernel(nb, west, east, to_prev, to_next, wide):
    pack_sides(nb, lambda s: west[s], lambda s: east[s], to_prev, to_next, wide)


def pack_ends(nb, above, below, from_prev, from_next, to_prev, to_next):
    position = lax.axis_index("tile")
    for slot, out, entry in ((0, to_prev, -1), (1, to_next, 1)):
        s = 2 * position + slot
        north = nb[slot, 0] == s + entry
        for i in range(3):
            top = above[slot, i].astype(F32)
            low = below[slot, 1 + i].astype(F32)
            out[64 * i : 64 * i + 64, :] = jnp.where(north, top, low).astype(BF)
        for side, strip in ((0, from_prev), (1, from_next)):
            for j in range(3):
                for edge in range(2):
                    at = 192 + 8 * (edge + 2 * (j + 3 * side))
                    out[at : at + 8, :] = strip[1 - slot, j, 56 * edge : 56 * edge + 8, :]


def window(shape, *index):
    return pl.BlockSpec(shape, lambda i: index)


SIDES = jax.ShapeDtypeStruct((2, 3, 64, 128), BF)
ENDS = jax.ShapeDtypeStruct((288, 128), BF)


def sides_of(nb, x):
    block = (2, 64, 8, 128)
    return call(
        sides_kernel,
        (SIDES, SIDES),
        [VMEM((2, 512, 128), F32)],
        (nb, x, x),
        1,
        blocks={1: window(block, 0, 0, 0, 0), 2: window(block, 0, 0, 7, 0)},
    )


def across(to_prev, to_next):
    columns = lax.axis_size("tile") // 4
    onward = [(4 * c + p, 4 * c + 7 - p) for c in range(columns - 1) for p in range(4)]
    back = [(b, a) for a, b in onward]
    onto = lax.ppermute(to_next, "tile", onward)
    return onto, lax.ppermute(to_prev, "tile", back)


def along(nb, x, from_prev, from_next):
    block = (2, 4, 64, 128)
    end_prev, end_next = call(
        pack_ends,
        (ENDS, ENDS),
        [],
        (nb, x, x, from_prev, from_next),
        1,
        blocks={1: window(block, 0, 0, 0, 0), 2: window(block, 0, 15, 0, 0)},
    )
    columns = lax.axis_size("tile") // 4
    down = [(4 * c + p, 4 * c + p + 1) for c in range(columns) for p in range(3)]
    up = [(b, a) for a, b in down]
    onto = lax.ppermute(end_next, "tile", down)
    return onto, lax.ppermute(end_prev, "tile", up)


def fill(nb, x, from_prev, from_next, chain_prev, chain_next, padded):
    position = lax.axis_index("tile")
    column = position // 4
    place = position % 4
    for slot in range(2):
        s = 2 * position + slot
        flat = padded.at[slot].reshape(70 * PITCH, 128)
        chain = chain_next if slot else chain_prev

        def body(i, carry):
            padded[slot, 3 + i, 8:72, :] = x[slot, i].astype(F32)
            return carry

        lax.fori_loop(0, 64, body, 0)
        for d, row, source in ((0, 0, 61), (1, 67, 0)):
            e = nb[slot, d]
            own = e == 2 * position + 1 - slot
            for i in range(3):
                mine = x[1 - slot, source + i].astype(F32)
                other = chain[64 * i : 64 * i + 64, :].astype(F32)
                value = jnp.where(own, mine, other)
                padded[slot, row + i, 8:72, :] = jnp.where(e >= 0, value, 0.0)
        for d, col in ((2, LEFT), (3, 72)):
            e = nb[slot, d]
            for j in range(3):
                value = jnp.where(
                    e < s,
                    from_prev[1 - slot, j].astype(F32),
                    from_next[1 - slot, j].astype(F32),
                )
                flat[pl.ds(3 * PITCH + col + j, 64, stride=PITCH), :] = jnp.where(
                    e >= 0, value, 0.0
                )
        for d, row, col, edge in (
            (4, 0, LEFT, 1),
            (5, 0, 72, 1),
            (6, 67, LEFT, 0),
            (7, 67, 72, 0),
        ):
            e = nb[slot, d]
            prev = e < s
            facing = jnp.where(prev, 8 * column - 2 - 2 * place, 8 * column + 14 - 2 * place)
            near = e == facing + slot
            for j in range(3):
                direct = jnp.where(
                    prev,
                    from_prev[slot, j, 56 * edge : 56 * edge + 8].astype(F32),
                    from_next[slot, j, 56 * edge : 56 * edge + 8].astype(F32),
                )
                at_prev = 192 + 8 * (edge + 2 * j)
                at_next = at_prev + 48
                relayed = jnp.where(
                    prev,
                    chain[at_prev : at_prev + 8].astype(F32),
                    chain[at_next : at_next + 8].astype(F32),
                )
                value = jnp.where(e >= 0, jnp.where(near, direct, relayed), 0.0)
                first = 5 if edge else 0
                for i in range(3):
                    at = (row + i) * PITCH + col + j
                    flat[at : at + 1, :] = value[first + i : first + i + 1]


def taps(padded, slot, kb, start, emit, flipped):
    def group(n, carry):
        row0 = 8 * (n // 4)
        col0 = pl.multiple_of(16 * (n % 4), 16)
        acc = [start(row0 + r, col0) for r in range(8)]
        for b in range(7):
            kk = [
                kb[(6 - a) * 7 + 6 - b] if flipped else kb[a * 7 + b] for a in range(7)
            ]
            for r in range(14):
                halves = [
                    padded[slot, row0 + r, pl.ds(col0 + (LEFT + b + 8 * h), 8), :]
                    for h in range(2)
                ]
                for a in range(7):
                    if 0 <= r - a < 8:
                        acc[r - a] = [acc[r - a][h] + halves[h] * kk[a] for h in range(2)]
        for r in range(8):
            emit(row0 + r, col0, acc[r])
        return carry

    lax.fori_loop(0, 32, group, 0)


def first_kernel(
    nb, ocean, x, from_prev, from_next, chain_prev, chain_next, cot, kb, cbias, wu, wd, wut, hbias,
    grad, to_prev, to_next, flat,
    padded, conv, nterm, aterm, sums, wide,
):
    fill(nb, x, from_prev, from_next, chain_prev, chain_next, padded)
    nterm[...] = jnp.zeros_like(nterm)
    aterm[...] = jnp.zeros_like(aterm)
    sums[...] = jnp.zeros_like(sums)
    ones = jnp.ones((16, 64 * RB), BF)

    def tile(slot):
        cb = jnp.broadcast_to(cbias[...], (8, 128))

        def keep(row, col0, value):
            for h in range(2):
                conv[row, pl.ds(col0 + 8 * h, 8), :] = value[h]

        taps(padded, slot, kb, lambda r, c: [cb, cb], keep, False)

        def block(at):
            value = conv[pl.ds(at, RB)].reshape(64 * RB, 128)
            ct = cot[slot, pl.ds(at, RB)].reshape(64 * RB, 128)
            mean = jnp.mean(value, -1, keepdims=True)
            centred = value - mean
            variance = jnp.mean(centred * centred, -1, keepdims=True)
            inverse = lax.rsqrt(variance + EPSILON)
            normed = centred * inverse
            nb16 = normed.astype(BF)
            left = jnp.concatenate([nb16.T, ones], 0)
            ctt = ct.T
            q = 0.0
            for part in range(2):
                cols = slice(256 * part, 256 * part + 256)
                h = jnp.dot(nb16, wu[:, cols], preferred_element_type=F32) + hbias[:, cols]
                ga = jnp.dot(ct, wd[:, cols], preferred_element_type=F32)
                act, gp = gelu_pair(h, ga)
                nterm[:, cols] += jnp.dot(left, gp, preferred_element_type=F32)
                aterm[:, cols] += jnp.dot(ctt, act, preferred_element_type=F32)
                q = q + jnp.dot(gp, wut[cols, :], preferred_element_type=F32)
            qm = q[:, 128:]
            q = q[:, :128]
            cross = jnp.mean(q * normed, -1, keepdims=True)
            gc = (inverse * (q - qm - normed * cross)).astype(BF)
            grad[slot, pl.ds(at, RB)] = gc.reshape(RB, 64, 128)
            sums[0:8] += jnp.sum(ct.astype(F32).reshape(8 * RB, 8, 128), 0)
            sums[8:16] += jnp.sum(gc.astype(F32).reshape(8 * RB, 8, 128), 0)

        def rows(i, carry):
            for u in range(UN):
                block(pl.multiple_of(RB * (UN * i + u), RB))
            return carry

        lax.fori_loop(0, 64 // (RB * UN), rows, 0)

    def step(slot, carry):
        pl.when(ocean[slot] > 0)(lambda: tile(slot))
        return carry

    lax.fori_loop(0, 2, step, 0)
    pack_sides(
        nb, lambda s: grad[s, :, 0:8, :], lambda s: grad[s, :, 56:64, :], to_prev, to_next, wide
    )
    for k in range(4):
        cols = slice(128 * k, 128 * k + 128)
        flat[cols] = nterm[0:128, cols]
        flat[512 + 128 * k : 640 + 128 * k] = aterm[:, cols]
        flat[1024 + k : 1025 + k] = nterm[128:129, cols]
    flat[1028:1029] = jnp.sum(sums[0:8], 0, keepdims=True)
    flat[1029:1030] = jnp.sum(sums[8:16], 0, keepdims=True)
    flat[1030:1152] = jnp.zeros((122, 128), F32)


def third_kernel(
    nb, ocean, flat_in, x, from_prev, from_next, chain_prev, chain_next, grad, flat,
    padded, gsc, kacc,
):
    fill(nb, x, from_prev, from_next, chain_prev, chain_next, padded)
    kacc[...] = jnp.zeros_like(kacc)

    def tile(slot):
        def widen(i, carry):
            gsc[i] = grad[slot, i].astype(F32)
            return carry

        lax.fori_loop(0, 64, widen, 0)

        def kgroup(n, carry):
            row0 = 8 * (n // 4)
            col0 = pl.multiple_of(16 * (n % 4), 16)
            g = [
                [gsc[row0 + r, pl.ds(col0 + 8 * h, 8), :] for h in range(2)] for r in range(8)
            ]
            for b in range(7):
                acc = [kacc[a * 7 + b] for a in range(7)]
                for r in range(14):
                    for h in range(2):
                        v = padded[slot, row0 + r, pl.ds(col0 + (LEFT + b + 8 * h), 8), :]
                        for a in range(7):
                            if 0 <= r - a < 8:
                                acc[a] = acc[a] + v * g[r - a][h]
                for a in range(7):
                    kacc[a * 7 + b] = acc[a]
            return carry

        lax.fori_loop(0, 32, kgroup, 0)

    def step(slot, carry):
        pl.when(ocean[slot] > 0)(lambda: tile(slot))
        return carry

    lax.fori_loop(0, 2, step, 0)
    flat[...] = flat_in[...]
    flat[1032:1081] = jnp.sum(kacc[...], 1)


def second_kernel(
    nb, ocean, g, from_prev, from_next, chain_prev, chain_next, cot, kb, out, padded
):
    fill(nb, g, from_prev, from_next, chain_prev, chain_next, padded)

    def step(slot, carry):
        def start(row, col0):
            both = cot[slot, row, pl.ds(col0, 16), :].astype(F32)
            return [both[:8], both[8:]]

        def emit(row, col0, value):
            both = jnp.concatenate(value, 0).astype(BF)
            out[slot, row, pl.ds(col0, 16), :] = both

        @pl.when(ocean[slot] > 0)
        def _():
            taps(padded, slot, kb, start, emit, True)

        @pl.when(ocean[slot] <= 0)
        def _():
            out[slot] = jnp.zeros((64, 64, 128), BF)

        return carry

    lax.fori_loop(0, 2, step, 0)


def whole(
    fields, cotangent, is_ocean, neighbours, kernel, conv_bias, ln_gain, ln_bias,
    w_up, up_bias, w_down, down_bias, layer_scale,
):
    x = fields[0]
    cot = cotangent[0]
    kb = jnp.broadcast_to(kernel.reshape(49, 1, 128), (49, 8, 128))
    upf = w_up.astype(F32)
    downf = w_down.astype(F32)
    gained = upf * ln_gain[:, None]
    wu = gained.astype(BF)
    wd = (downf * layer_scale[None, :]).T.astype(BF)
    mean_row = jnp.mean(gained, 0)
    wut = jnp.concatenate(
        [gained.T, jnp.broadcast_to(mean_row[:, None], (512, 128))], 1
    ).astype(BF)
    hbias = (up_bias + jnp.dot(ln_bias, upf, precision="highest"))[None]
    sides = across(*sides_of(neighbours, x))
    halos = (*sides, *along(neighbours, x, *sides))
    sd = jax.ShapeDtypeStruct
    pad = VMEM((2, 70, PITCH, 128), F32)
    grad, to_prev, to_next, flat = call(
        first_kernel,
        (sd((2, 64, 64, 128), BF), SIDES, SIDES, sd((1152, 128), F32)),
        [
            pad,
            VMEM((64, 64, 128), F32),
            VMEM((144, 512), F32),
            VMEM((128, 512), F32),
            VMEM((16, 128), F32),
            VMEM((2, 512, 128), F32),
        ],
        (neighbours, is_ocean, x, *halos, cot, kb, conv_bias[None], wu, wd, wut, hbias),
        2,
        flops=2 * 10**10,
        bytes_accessed=10**7,
    )
    sides = across(to_prev, to_next)
    flat = call(
        third_kernel,
        sd((1152, 128), F32),
        [pad, VMEM((64, 64, 128), F32), VMEM((49, 8, 128), F32)],
        (neighbours, is_ocean, flat, x, *halos, grad),
        2,
        flops=10**10,
        bytes_accessed=10**7,
        alias={2: 0},
    )
    halos_g = (*sides, *along(neighbours, grad, *sides))
    out = call(
        second_kernel,
        sd((2, 64, 64, 128), BF),
        [pad],
        (neighbours, is_ocean, grad, *halos_g, cot, kb),
        2,
        flops=10**10,
        bytes_accessed=10**7,
    )
    n = lax.axis_size("tile") * lax.axis_size("dp")
    axes = ("tile", "dp")
    got = lax.all_to_all(flat.reshape(n, 1, 1152 * 128 // n), axes, 0, 0, tiled=True)
    mine = jnp.sum(got, 0)
    spread = jnp.broadcast_to(mine[None], (n, *mine.shape))
    flat = lax.all_to_all(spread, axes, 0, 0, tiled=True).reshape(1152, 128)
    scale = 1.0 / math.sqrt(
        fields.shape[0]
        * lax.axis_size("dp")
        * fields.shape[1]
        * lax.axis_size("tile")
        * fields.shape[2] ** 2
    )
    row = sd((1, 128), F32)
    rows = jnp.stack([ln_gain, ln_bias, layer_scale, down_bias])
    done = call(
        partial(finish_kernel, scale),
        (
            sd((7, 7, 128), F32),
            row,
            row,
            row,
            sd((128, 512), F32),
            sd((1, 512), F32),
            sd((512, 128), F32),
            row,
            row,
        ),
        [],
        (flat, rows, w_up, w_down),
        0,
    )
    done = [d[0] if d.shape[0] == 1 else d for d in done]
    return (out[None], *done)


def finish_kernel(
    scale, flat, rows, w_up, w_down,
    g_kernel, g_conv_bias, g_ln_gain, g_ln_bias, g_w_up, g_up_bias, g_w_down, g_down_bias,
    g_layer_scale,
):
    square = (128, 128)
    gain = jnp.broadcast_to(rows[0:1], square).T
    bias = jnp.broadcast_to(rows[1:2], square).T
    layer = rows[2:3]
    cot_sum = flat[1028:1029] * scale
    gains = jnp.zeros(square, F32)
    biases = jnp.zeros(square, F32)
    layers = jnp.zeros(square, F32)
    for k in range(4):
        cols = slice(128 * k, 128 * k + 128)
        upper = w_up[:, cols].astype(F32)
        n = flat[cols] * scale
        a = flat[512 + 128 * k : 640 + 128 * k].T * scale
        up = flat[1024 + k : 1025 + k] * scale
        g_w_up[:, cols] = n * gain + bias * up
        g_up_bias[:, cols] = up
        g_w_down[cols, :] = a * layer
        gains = gains + n * upper
        biases = biases + upper * up
        layers = layers + a * w_down[cols, :].astype(F32)
    g_ln_gain[...] = jnp.sum(gains.T, 0, keepdims=True)
    g_ln_bias[...] = jnp.sum(biases.T, 0, keepdims=True)
    g_layer_scale[...] = jnp.sum(layers, 0, keepdims=True) + rows[3:4] * cot_sum
    g_down_bias[...] = layer * cot_sum
    g_conv_bias[...] = flat[1029:1030] * scale
    for i in range(7):
        g_kernel[i] = flat[1032 + 7 * i : 1039 + 7 * i] * scale


def solution(mesh):
    placed = (
        P("dp", "tile", None, None, None),
        P("dp", "tile", None, None, None),
        P("tile"),
        P("tile", None),
    ) + (P(),) * 9
    return jax.shard_map(
        whole,
        mesh=mesh,
        in_specs=placed,
        out_specs=(P("dp", "tile", None, None, None),) + (P(),) * 9,
        check_vma=False,
    )
```
